128 devices in a mesh: group: 16 (over x, z), local: 8 (over y, core).
Axes of the slice: x: 4, y: 4, z: 4, core: 2. Of those that a mesh axis runs over, the one named last changes fastest.
Arguments:
- ids: int32 [16384, 128, 8], P(('group', 'local')), may hold values from 0 to 4095
- lengths: int32 [16384, 128], P(('group', 'local')), may hold values from 1 to 8, as said below
- id_weights: float32 [16384, 128, 8], P(('group', 'local')), may hold values from 0.5 to 1.5
- table: float32 [524288, 256], P(('group', 'local')), may hold values from -2.4 to 2.4
Outputs:
- pooled: float32 [16384, 128, 256], P(('group', 'local'))
The draws below stay inside these ranges and needn't reach their ends.
Inputs may be any that keep to these rules, and one draw needn't show every extreme that they name: `lengths`: every draw has some bag with 8 live ids.
All inputs are finite; a program needn't handle non-finite values.
Results may differ from the reference program's by a relative error of at most 0.00002.
Values sent between devices are 32-bit elements; how exact they have to be, the bound alone decides.
A program may use at most 128 MiB of HBM per device.

```python
import math
import jax
import jax.numpy as jnp
import numpy as np
from jax import lax

DIM = 256
BAG = 8
EX_DEV = 128
ROWS = 4096
TABLES = 128
EXAMPLES = 16384
DEVICES = 128


def draw_lengths(key, part):
    first, second, third, fourth = jax.random.split(jax.random.fold_in(key, 17), 4)
    limits = jax.random.randint(first, (TABLES,), BAG // 2, BAG + 1)
    busiest = jax.random.randint(second, (), 0, TABLES)
    columns = jnp.arange(TABLES)
    limits = jnp.where(columns == busiest, BAG, limits)
    spread = (limits + 1) // 2
    counts = limits[None, :] - jax.random.randint(third, (EXAMPLES, TABLES), 0, BAG) % spread[None, :]
    chosen = jax.random.randint(fourth, (), 0, EXAMPLES)
    spot = (jnp.arange(EXAMPLES)[:, None] == chosen) & (columns[None, :] == busiest)
    counts = jnp.where(spot, BAG, counts)
    return counts.astype(jnp.int32)


def plant(drawn, stream_key, low, top_value):
    longest = drawn.shape.index(max(drawn.shape))
    spots = []
    for shift in (0, 1):
        where = [jax.random.randint(jax.random.fold_in(stream_key, axis), (), 0, length) for axis, length in enumerate(drawn.shape)]
        where[longest] = (where[longest] + shift) % drawn.shape[longest]
        spots.append(tuple(where))
    return drawn.at[spots[0]].set(low).at[spots[1]].set(top_value)


def steps_of(key, shape, shards, low, top_value):
    factor_of, own = 1.0, jax.random.fold_in(key, 6)
    for dim, parts in shards:
        draws = jnp.exp(jax.random.uniform(jax.random.fold_in(own, dim), (parts,), jnp.float32, low / len(shards), top_value / len(shards)))
        factor_of = factor_of * jnp.repeat(draws, shape[dim] // parts).reshape([-1 if axis == dim else 1 for axis in range(len(shape))])
    return factor_of


def rank_bounds(amount, lean):
    weights = [(1 << 20) // math.isqrt(rank ** lean) + 1 for rank in range(1, amount + 1)]
    deviation = 1 + sum(weights) // (1 << 30)
    return np.cumsum(np.array([max(1, weight // deviation) for weight in weights]))


def ranked(own_key, dims, amount, skew):
    listing = rank_bounds(amount, skew)
    lot = jax.random.randint(jax.random.fold_in(own_key, 1), dims, 0, int(listing[amount - 1]))
    standing = jnp.searchsorted(jnp.asarray(listing, jnp.int32), lot, side="right")
    return jax.random.permutation(jax.random.fold_in(own_key, 2), amount)[standing].astype(jnp.int32)


def gaussian(key, shape, width, most, pieces=(), kind=jnp.bfloat16):
    values = jax.random.normal(key, shape, jnp.float32) * width
    if len(pieces) > 0:
        values = steps_of(key, shape, pieces, -0.22, 0.18) * values
    return jnp.clip(values, min=-most, max=most).astype(kind)


def setup_inputs(seed: int = 0) -> dict:
    keys = jax.random.split(jax.random.key(seed), 5)
    return {
        "ids": plant(ranked(keys[0], (EXAMPLES, TABLES, BAG), ROWS, 2), jax.random.fold_in(keys[0], 3), 0, ROWS - 1).astype(jnp.int32),
        "lengths": draw_lengths(jax.random.fold_in(keys[4], 71), 0),
        "id_weights": jnp.clip(0.5 + 1.0 * jax.random.uniform(keys[2], (EXAMPLES, TABLES, BAG), jnp.float32) ** steps_of(keys[2], (EXAMPLES, TABLES, BAG), ((0, 128),), -0.2, 0.2), 0.5, 1.5),
        "table": gaussian(keys[3], (TABLES * ROWS, DIM), 0.3, 2.4, ((0, 128),), jnp.float32),
    }


def reference(ids, lengths, id_weights, table):
    slot = lax.broadcasted_iota(jnp.int32, ids.shape, 2)
    masked = jnp.where(slot < lengths[:, :, None], id_weights, jnp.zeros_like(id_weights))
    offsets = (jnp.arange(TABLES, dtype=jnp.int32) * ROWS).astype(jnp.int32)
    index = (ids + offsets[None, :, None]).astype(jnp.int32)
    index = jnp.transpose(index, (1, 0, 2)).reshape(TABLES, DEVICES, EX_DEV, BAG)
    weights = jnp.transpose(masked, (1, 0, 2)).reshape(TABLES, DEVICES, EX_DEV, BAG)

    def one_block(pair):
        rows = jnp.take(table, pair[0], axis=0)
        return jnp.sum(rows * pair[1][:, :, None], axis=1)

    def one_table(pair):
        return lax.map(one_block, pair)

    result = lax.map(one_table, (index, weights))
    result = result.reshape(TABLES, EXAMPLES, DIM)
    return jnp.transpose(result, (1, 0, 2))
```

```python
import functools

import jax
import jax.numpy as jnp
from jax import lax
from jax.experimental import pallas as pl
from jax.experimental.pallas import tpu as pltpu
from jax.sharding import PartitionSpec as P

MESH = pl.DeviceIdType.MESH
ANY = pl.BlockSpec(memory_space=pl.ANY)
SPEC = P(("group", "local"))


def pool_send_kernel(bags, ids_hbm, w_hbm, table_hbm, out_hbm, table, obuf, wbuf, ids, in_sem, id_sem, send_sem, recv_sem, own_sem):
    g, l = lax.axis_index("group"), lax.axis_index("local")
    me = g * 8 + l
    peers = ids_hbm.shape[0]
    chunks = ids_hbm.shape[1]
    lanes = ids_hbm.shape[2]
    bag = lanes // bags
    rows = 2 * bags

    table_copy = pltpu.make_async_copy(table_hbm, table, in_sem.at[0])
    w_copy = pltpu.make_async_copy(w_hbm, wbuf, in_sem.at[1])
    table_copy.start()
    w_copy.start()

    def ids_copy(ch):
        return pltpu.make_async_copy(ids_hbm.at[:, ch, :], ids.at[ch % 2], id_sem.at[ch % 2])

    ids_copy(0).start()

    barrier = pltpu.get_barrier_semaphore()

    def greet(k, _):
        d = (me + k) % peers
        pl.semaphore_signal(barrier, inc=1, device_id=(d // 8, d % 8), device_id_type=MESH)
        return 0

    lax.fori_loop(1, peers, greet, 0)
    pl.semaphore_wait(barrier, peers - 1)
    table_copy.wait()
    w_copy.wait()

    def target(k):
        q = (k * 37) % peers
        x = (g // 4 + q // 32) % 4
        z = (g % 4 + (q // 8) % 4) % 4
        y = (l // 2 + (q // 2) % 4) % 4
        c = (l % 2 + q % 2) % 2
        return x * 4 + z, y * 2 + c

    def pool(ch, d):
        slot = ch % 2
        w = jnp.broadcast_to(wbuf[d, pl.ds(ch, 1), :], (2, lanes))
        for e in range(bags):
            total = None
            for j in range(bag):
                q = e * bag + j
                row = table[pl.ds(ids[slot, d, q], 2), :]
                term = row * jnp.broadcast_to(w[:, q : q + 1], (2, lanes))
                total = term if total is None else total + term
            obuf[d, ch, pl.ds(2 * e, 2), :] = total

    def do_chunk(ch, _):
        ids_copy(ch).wait()

        @pl.when(ch + 1 < chunks)
        def _():
            ids_copy(ch + 1).start()

        def do_peer(k, _):
            tg, tl = target(k)
            d = tg * 8 + tl
            pool(ch, d)
            pltpu.make_async_remote_copy(
                obuf.at[d, ch], out_hbm.at[me, ch], send_sem, recv_sem, device_id=(tg, tl), device_id_type=MESH
            ).start()
            return 0

        lax.fori_loop(1, peers, do_peer, 0)
        pool(ch, me)
        return 0

    lax.fori_loop(0, chunks, do_chunk, 0)
    own = pltpu.make_async_copy(obuf.at[me], out_hbm.at[me], own_sem)
    own.start()
    own.wait()
    got = out_hbm.at[pl.ds(0, peers - 1)]
    pltpu.make_async_copy(got, got, send_sem).wait()
    pltpu.make_async_copy(got, got, recv_sem).wait()


def body(ids, lengths, id_weights, table):
    examples, tables, bag = ids.shape
    bags = 128 // bag
    chunks = examples // bags
    rows = table.shape[0]
    slot = lax.broadcasted_iota(jnp.int32, ids.shape, 2)
    masked = jnp.where(slot < lengths[:, :, None], id_weights, jnp.zeros_like(id_weights))

    def by_table(v):
        return jnp.transpose(v, (1, 0, 2)).reshape(tables, 1, chunks, 128)

    packed = jnp.concatenate([by_table(ids.astype(jnp.float32)), by_table(masked)], axis=1)
    arrived = lax.all_to_all(packed, ("group", "local"), split_axis=0, concat_axis=0, tiled=True)
    index = arrived[:, 0].astype(jnp.int32) * 2
    weights = arrived[:, 1]
    flat = table.reshape(rows * 2, 128)
    got = pl.pallas_call(
        functools.partial(pool_send_kernel, bags),
        out_shape=jax.ShapeDtypeStruct((tables, chunks, 2 * bags, 128), jnp.float32),
        in_specs=[ANY, ANY, ANY],
        out_specs=ANY,
        scratch_shapes=[
            pltpu.VMEM((rows * 2, 128), jnp.float32),
            pltpu.VMEM((tables, chunks, 2 * bags, 128), jnp.float32),
            pltpu.VMEM((tables, chunks, 128), jnp.float32),
            pltpu.SMEM((2, tables, 128), jnp.int32),
            pltpu.SemaphoreType.DMA((2,)),
            pltpu.SemaphoreType.DMA((2,)),
            pltpu.SemaphoreType.DMA,
            pltpu.SemaphoreType.DMA,
            pltpu.SemaphoreType.DMA,
        ],
        compiler_params=pltpu.CompilerParams(vmem_limit_bytes=40 << 20, collective_id=0, has_side_effects=True),
        name="pool_send",
    )(index, weights, flat)
    return jnp.transpose(got.reshape(tables, examples, 256), (1, 0, 2))


def solution(mesh):
    return jax.shard_map(body, mesh=mesh, in_specs=(SPEC,) * 4, out_specs=SPEC, check_vma=False)
```

```python
import functools

import jax
import jax.numpy as jnp
from jax import lax
from jax.experimental import pallas as pl
from jax.experimental.pallas import tpu as pltpu
from jax.sharding import PartitionSpec as P

MESH = pl.DeviceIdType.MESH
ANY = pl.BlockSpec(memory_space=pl.ANY)
SPEC = P(("group", "local"))
LANES = 128
BAG = 8
BAGS = 16
PAD = 8


def pool_send_kernel(ids_hbm, w_hbm, table_hbm, out_hbm, table, obuf, ids_v, wbuf, ids, in_sem, id_sem, send_sem, recv_sem, own_sem):
    g, l = lax.axis_index("group"), lax.axis_index("local")
    me = g * 8 + l
    peers = out_hbm.shape[0]
    pieces = out_hbm.shape[1]
    groups = peers // 8
    steps = pieces * groups

    rows = table_hbm.shape[0]
    table_copy = pltpu.make_async_copy(table_hbm, table.at[pl.ds(PAD, rows)], in_sem.at[0])
    w_copy = pltpu.make_async_copy(w_hbm, wbuf, in_sem.at[1])
    i_copy = pltpu.make_async_copy(ids_hbm, ids_v, in_sem.at[2])
    i_copy.start()
    table_copy.start()
    w_copy.start()
    table[pl.ds(0, PAD), :] = jnp.zeros((PAD, LANES), jnp.float32)
    table[pl.ds(PAD + rows, PAD), :] = jnp.zeros((PAD, LANES), jnp.float32)

    barrier = pltpu.get_barrier_semaphore()

    def greet(k, _):
        d = lax.rem(me + k, peers)
        pl.semaphore_signal(barrier, inc=1, device_id=(lax.div(d, 8), lax.rem(d, 8)), device_id_type=MESH)
        return 0

    lax.fori_loop(1, peers, greet, 0)
    i_copy.wait()

    gx, gz = lax.div(g, 4), lax.rem(g, 4)

    def piece_group(i):
        ch = lax.div(i, groups)
        q = lax.rem(i * 5 + ch * 3, groups)
        return ch, lax.rem(gx + lax.div(q, 4), 4) * 4 + lax.rem(gz + lax.rem(q, 4), 4)

    def ids_copy(i, slot):
        ch, tg = piece_group(i)
        return pltpu.make_async_copy(ids_v.at[ch, pl.ds(tg * 8, 8)], ids.at[slot], id_sem.at[slot])

    ids_copy(0, 0).start()
    ids_copy(1, 1).start()
    pl.semaphore_wait(barrier, peers - 1)
    table_copy.wait()
    w_copy.wait()

    quarter = lax.broadcasted_iota(jnp.int32, (8, LANES), 0) // 2

    def pool(slot, tl, d, ch):
        shift = lax.rem(128 - lax.rem(ch, 4) * 32, 128)
        w = pltpu.roll(wbuf[d, lax.div(ch, 4)], shift, 1)
        for quad in range(BAGS // 4):
            total = None
            for j in range(BAG):
                row = None
                for a in range(4):
                    one = table[pl.ds(ids[slot, tl, (quad * 4 + a) * BAG + j], 8), :]
                    row = one if a == 0 else jnp.where(quarter == a, one, row)
                q = quad * BAG + j
                term = row * jnp.broadcast_to(w[:, q : q + 1], (8, LANES))
                total = term if total is None else total + term
            obuf[d, ch, pl.ds(8 * quad, 8), :] = total

    def step(t, _):
        for slot in range(2):
            i = t * 2 + slot
            ch, tg = piece_group(i)
            ids_copy(i, slot).wait()
            for tl in range(8):
                d = tg * 8 + tl
                pool(slot, tl, d, ch)

                @pl.when(d != me)
                def _():
                    pltpu.make_async_remote_copy(
                        obuf.at[d, ch], out_hbm.at[me, ch], send_sem, recv_sem, device_id=(tg, tl), device_id_type=MESH
                    ).start()

            @pl.when(i + 2 < steps)
            def _():
                ids_copy(i + 2, slot).start()

        return 0

    lax.fori_loop(0, steps // 2, step, 0)
    own = pltpu.make_async_copy(obuf.at[me], out_hbm.at[me], own_sem)
    own.start()
    own.wait()
    got = out_hbm.at[pl.ds(0, peers - 1)]
    pltpu.make_async_copy(got, got, send_sem).wait()
    pltpu.make_async_copy(got, got, recv_sem).wait()


def body(ids, lengths, id_weights, table):
    examples, tables, bag = ids.shape
    pieces = examples // BAGS
    rows = table.shape[0]
    slot = lax.broadcasted_iota(jnp.int32, ids.shape, 2)
    masked = jnp.where(slot < lengths[:, :, None], id_weights, jnp.zeros_like(id_weights))

    def by_table(v):
        return jnp.transpose(v, (1, 0, 2)).reshape(tables, 1, pieces, LANES)

    packed = jnp.concatenate([by_table(ids.astype(jnp.float32)), by_table(masked)], axis=1)
    arrived = lax.all_to_all(packed, ("group", "local"), split_axis=0, concat_axis=0, tiled=True)
    place = lax.broadcasted_iota(jnp.int32, (1, 1, LANES), 2) // BAG % 4
    index = jnp.transpose(arrived[:, 0].astype(jnp.int32), (1, 0, 2)) * 2 + (PAD - 2 * place)
    weights = arrived[:, 1].reshape(tables, 2, 4, 4, 4, BAG)
    weights = jnp.transpose(weights, (0, 1, 4, 2, 3, 5)).reshape(tables, 2, 4, 1, LANES)
    weights = jnp.broadcast_to(weights, (tables, 2, 4, 2, LANES)).reshape(tables, 2, 8, LANES)
    flat = table.reshape(rows * 2, LANES)
    got = pl.pallas_call(
        pool_send_kernel,
        out_shape=jax.ShapeDtypeStruct((tables, pieces, 2 * BAGS, LANES), jnp.float32),
        in_specs=[ANY, ANY, ANY],
        out_specs=ANY,
        scratch_shapes=[
            pltpu.VMEM((rows * 2 + 2 * PAD, LANES), jnp.float32),
            pltpu.VMEM((tables, pieces, 2 * BAGS, LANES), jnp.float32),
            pltpu.VMEM((pieces, tables, LANES), jnp.int32),
            pltpu.VMEM((tables, 2, 8, LANES), jnp.float32),
            pltpu.SMEM((2, 8, LANES), jnp.int32),
            pltpu.SemaphoreType.DMA((3,)),
            pltpu.SemaphoreType.DMA((2,)),
            pltpu.SemaphoreType.DMA,
            pltpu.SemaphoreType.DMA,
            pltpu.SemaphoreType.DMA,
        ],
        compiler_params=pltpu.CompilerParams(vmem_limit_bytes=40 << 20, collective_id=0, has_side_effects=True),
        name="pool_send",
    )(index, weights, flat)
    return jnp.transpose(got.reshape(tables, examples, 256), (1, 0, 2))


def solution(mesh):
    return jax.shard_map(body, mesh=mesh, in_specs=(SPEC,) * 4, out_specs=SPEC, check_vma=False)
```

```python
import jax
import jax.numpy as jnp
from jax import lax
from jax.experimental import pallas as pl
from jax.experimental.pallas import tpu as pltpu
from jax.sharding import PartitionSpec as P

MESH = pl.DeviceIdType.MESH
ANY = pl.BlockSpec(memory_space=pl.ANY)
HBM = pl.BlockSpec(memory_space=pltpu.HBM)
VMEM = pl.BlockSpec(memory_space=pltpu.VMEM)
SPEC = P(("group", "local"))
LANES = 128
BAG = 8
BAGS = 16
PAD = 8


def pool_send_kernel(
    ids_in, w_in, table_hbm, got, raw, table, obuf, ids_v, w_v, ids, raw_sem, stage_sem, ask_sem, ids_sem, w_sem, send_sem, recv_sem
):
    g, l = lax.axis_index("group"), lax.axis_index("local")
    me = g * 8 + l
    pieces, peers = got.shape[0], got.shape[2]
    groups = peers // 8
    steps = pieces * groups
    rows = table_hbm.shape[0]

    raw_copy = pltpu.make_async_copy(table_hbm, raw, raw_sem)
    raw_copy.start()

    barrier = pltpu.get_barrier_semaphore()

    def greet(k, _):
        d = lax.rem(me + k, peers)
        pl.semaphore_signal(barrier, inc=1, device_id=(lax.div(d, 8), lax.rem(d, 8)), device_id_type=MESH)
        return 0

    lax.fori_loop(1, peers, greet, 0)

    gx, gz = lax.div(g, 4), lax.rem(g, 4)
    pltpu.make_async_copy(ids_in.at[me], ids_v.at[me], ids_sem.at[g]).start()
    pltpu.make_async_copy(w_in.at[me], w_v.at[me], w_sem.at[g]).start()
    pl.semaphore_wait(barrier, peers - 1)

    def ask(i, _):
        q = lax.rem(i * 5, groups)
        tg = lax.rem(gx + 4 - lax.div(q, 4), 4) * 4 + lax.rem(gz + 4 - lax.rem(q, 4), 4)
        for tl in range(8):
            d = tg * 8 + tl

            @pl.when(d != me)
            def _():
                to = dict(device_id=(tg, tl), device_id_type=MESH)
                pltpu.make_async_remote_copy(ids_in.at[d], ids_v.at[me], ask_sem, ids_sem.at[g], **to).start()
                pltpu.make_async_remote_copy(w_in.at[d], w_v.at[me], ask_sem, w_sem.at[g], **to).start()

        return 0

    lax.fori_loop(0, groups, ask, 0)

    table[pl.ds(0, PAD), :] = jnp.zeros((PAD, LANES), jnp.float32)
    table[pl.ds(PAD + 2 * rows, PAD), :] = jnp.zeros((PAD, LANES), jnp.float32)
    raw_copy.wait()

    def lay(t, _):
        for u in range(8):
            r = pl.multiple_of((t * 8 + u) * 8, 8)
            for h in range(2):
                table[pl.ds(PAD + 2 * r + h, 8, stride=2), :] = raw[pl.ds(r, 8), pl.ds(h * LANES, LANES)]
        return 0

    lax.fori_loop(0, rows // 64, lay, 0)

    def piece_group(i):
        ch = lax.div(i, groups)
        q = lax.rem(i * 5 + ch * 3, groups)
        return ch, lax.rem(gx + lax.div(q, 4), 4) * 4 + lax.rem(gz + lax.rem(q, 4), 4)

    def stage(i, slot):
        ch, tg = piece_group(i)
        return pltpu.make_async_copy(ids_v.at[pl.ds(tg * 8, 8), ch], ids.at[slot], stage_sem.at[slot])

    def stage_next(i, slot):
        @pl.when(i < groups)
        def _():
            _, tg = piece_group(i)
            block = ids_v.at[pl.ds(tg * 8, 8)]
            pltpu.make_async_copy(block, block, ids_sem.at[tg]).wait()
            block = w_v.at[pl.ds(tg * 8, 8)]
            pltpu.make_async_copy(block, block, w_sem.at[tg]).wait()

        stage(i, slot).start()

    stage_next(0, 0)
    stage_next(1, 1)

    quarter = lax.broadcasted_iota(jnp.int32, (8, LANES), 0) // 2

    def by_quarter(parts):
        row = parts[0]
        for a in range(1, 4):
            row = jnp.where(quarter == a, parts[a], row)
        return row

    def pool(slot, tl, d, ch):
        shift = lax.rem(128 - lax.rem(ch, 4) * 32, 128)
        half = lax.div(ch, 4) * 4
        w = by_quarter([jnp.broadcast_to(w_v[d, pl.ds(half + a, 1), :], (8, LANES)) for a in range(4)])
        w = pltpu.roll(w, shift, 1)
        for quad in range(BAGS // 4):
            total = None
            for j in range(BAG):
                row = by_quarter([table[pl.ds(ids[slot, tl, (quad * 4 + a) * BAG + j], 8), :] for a in range(4)])
                q = quad * BAG + j
                term = row * jnp.broadcast_to(w[:, q : q + 1], (8, LANES))
                total = term if total is None else total + term
            obuf[d, ch, pl.ds(8 * quad, 8), :] = total

    def step(t, _):
        for slot in range(2):
            i = t * 2 + slot
            ch, tg = piece_group(i)
            stage(i, slot).wait()
            for tl in range(8):
                d = tg * 8 + tl
                pool(slot, tl, d, ch)

                @pl.when(d != me)
                def _():
                    pltpu.make_async_remote_copy(
                        obuf.at[d, ch], got.at[ch, :, me], send_sem, recv_sem, device_id=(tg, tl), device_id_type=MESH
                    ).start()

            @pl.when(i + 2 < steps)
            def _():
                stage_next(i + 2, slot)

        return 0

    lax.fori_loop(0, steps // 2, step, 0)
    pltpu.make_async_copy(obuf.at[me], got.at[:, :, me], recv_sem).start()
    sent = obuf.at[pl.ds(0, peers - 1)]
    pltpu.make_async_copy(sent, sent, send_sem).wait()
    asked = ids_v.at[pl.ds(0, peers - 1)]
    pltpu.make_async_copy(asked, asked, ask_sem).wait()
    pltpu.make_async_copy(asked, asked, ask_sem).wait()
    pltpu.make_async_copy(got, got, recv_sem).wait()


def place_kernel(got, out_hbm, sem):
    examples = out_hbm.shape[0]
    parts = sem.shape[0]
    batch = examples // parts

    def copy(p, h):
        cut = pl.ds(p * batch, batch)
        return pltpu.make_async_copy(got.at[cut, h], out_hbm.at[cut, :, pl.ds(h * LANES, LANES)], sem.at[p, h])

    for p in range(parts):
        for h in range(2):
            copy(p, h).start()
    for p in range(parts):
        for h in range(2):
            copy(p, h).wait()


def body(ids, lengths, id_weights, table):
    examples, tables, bag = ids.shape
    pieces = examples // BAGS
    rows, width = table.shape
    slot = lax.broadcasted_iota(jnp.int32, ids.shape, 2)
    masked = jnp.where(slot < lengths[:, :, None], id_weights, jnp.zeros_like(id_weights))

    place = lax.broadcasted_iota(jnp.int32, (1, 1, LANES), 2) // BAG % 4
    index = jnp.transpose(ids, (1, 0, 2)).reshape(tables, pieces, LANES) * 2 + (PAD - 2 * place)
    weights = masked.reshape(2, 4, 4, 4, tables, bag)
    weights = jnp.transpose(weights, (4, 0, 3, 1, 2, 5)).reshape(tables, 8, LANES)
    got = pl.pallas_call(
        pool_send_kernel,
        out_shape=pltpu.VMEM((pieces, 2 * BAGS, tables, LANES), jnp.float32),
        in_specs=[ANY, ANY, HBM],
        out_specs=VMEM,
        scratch_shapes=[
            pltpu.VMEM((rows, width), jnp.float32),
            pltpu.VMEM((rows * 2 + 2 * PAD, LANES), jnp.float32),
            pltpu.VMEM((tables, pieces, 2 * BAGS, LANES), jnp.float32),
            pltpu.VMEM((tables, pieces, LANES), jnp.int32),
            pltpu.VMEM((tables, 8, LANES), jnp.float32),
            pltpu.SMEM((2, 8, LANES), jnp.int32),
            pltpu.SemaphoreType.DMA,
            pltpu.SemaphoreType.DMA((2,)),
            pltpu.SemaphoreType.DMA,
            pltpu.SemaphoreType.DMA((tables // 8,)),
            pltpu.SemaphoreType.DMA((tables // 8,)),
            pltpu.SemaphoreType.DMA,
            pltpu.SemaphoreType.DMA,
        ],
        compiler_params=pltpu.CompilerParams(vmem_limit_bytes=44 << 20, collective_id=0, has_side_effects=True),
        name="pool_send",
    )(index, weights, table)
    return pl.pallas_call(
        place_kernel,
        out_shape=jax.ShapeDtypeStruct((examples, tables, width), jnp.float32),
        in_specs=[VMEM],
        out_specs=ANY,
        scratch_shapes=[pltpu.SemaphoreType.DMA((8, 2))],
        compiler_params=pltpu.CompilerParams(vmem_limit_bytes=20 << 20),
        name="place",
    )(got.reshape(examples, 2, tables, LANES))


def solution(mesh):
    return jax.shard_map(body, mesh=mesh, in_specs=(SPEC,) * 4, out_specs=SPEC, check_vma=False)
```

```python
import jax
import jax.numpy as jnp
from jax import lax
from jax.experimental import pallas as pl
from jax.experimental.pallas import tpu as pltpu
from jax.sharding import PartitionSpec as P

MESH = pl.DeviceIdType.MESH
ANY = pl.BlockSpec(memory_space=pl.ANY)
HBM = pl.BlockSpec(memory_space=pltpu.HBM)
VMEM = pl.BlockSpec(memory_space=pltpu.VMEM)
SPEC = P(("group", "local"))
LANES = 128
BAG = 8
BAGS = 16
GAP = 8


def pool_send_kernel(
    ids_in, w_in, table_hbm, got, table, obuf, ids_v, w_v, ids, table_sem, stage_sem, ask_sem, ids_sem, w_sem, send_sem, recv_sem
):
    g, l = lax.axis_index("group"), lax.axis_index("local")
    me = g * 8 + l
    pieces, peers = got.shape[0], got.shape[2]
    groups = peers // 8
    steps = pieces * groups
    rows = table_hbm.shape[0]

    halves = [
        pltpu.make_async_copy(
            table_hbm.at[:, pl.ds(h * LANES, LANES)], table.at[pl.ds(h * (rows + GAP), rows)], table_sem.at[h]
        )
        for h in range(2)
    ]
    for half in halves:
        half.start()

    barrier = pltpu.get_barrier_semaphore()

    def greet(k, _):
        d = lax.rem(me + k, peers)
        pl.semaphore_signal(barrier, inc=1, device_id=(lax.div(d, 8), lax.rem(d, 8)), device_id_type=MESH)
        return 0

    lax.fori_loop(1, peers, greet, 0)

    gx, gz = lax.div(g, 4), lax.rem(g, 4)
    pltpu.make_async_copy(ids_in.at[me], ids_v.at[me], ids_sem.at[g]).start()
    pltpu.make_async_copy(w_in.at[me], w_v.at[me], w_sem.at[g]).start()
    pl.semaphore_wait(barrier, peers - 1)

    def ask(i, _):
        q = lax.rem(i * 5, groups)
        tg = lax.rem(gx + 4 - lax.div(q, 4), 4) * 4 + lax.rem(gz + 4 - lax.rem(q, 4), 4)
        for tl in range(8):
            d = tg * 8 + tl

            @pl.when(d != me)
            def _():
                to = dict(device_id=(tg, tl), device_id_type=MESH)
                pltpu.make_async_remote_copy(ids_in.at[d], ids_v.at[me], ask_sem, ids_sem.at[g], **to).start()
                pltpu.make_async_remote_copy(w_in.at[d], w_v.at[me], ask_sem, w_sem.at[g], **to).start()

        return 0

    lax.fori_loop(0, groups, ask, 0)

    for half in halves:
        half.wait()

    def piece_group(i):
        ch = lax.div(i, groups)
        q = lax.rem(i * 5 + ch * 3, groups)
        return ch, lax.rem(gx + lax.div(q, 4), 4) * 4 + lax.rem(gz + lax.rem(q, 4), 4)

    def stage(i, slot):
        ch, tg = piece_group(i)
        return pltpu.make_async_copy(ids_v.at[pl.ds(tg * 8, 8), ch], ids.at[slot], stage_sem.at[slot])

    def stage_next(i, slot):
        @pl.when(i < groups)
        def _():
            _, tg = piece_group(i)
            block = ids_v.at[pl.ds(tg * 8, 8)]
            pltpu.make_async_copy(block, block, ids_sem.at[tg]).wait()
            block = w_v.at[pl.ds(tg * 8, 8)]
            pltpu.make_async_copy(block, block, w_sem.at[tg]).wait()

        stage(i, slot).start()

    stage_next(0, 0)
    stage_next(1, 1)

    sublane = lax.broadcasted_iota(jnp.int32, (8, LANES), 0)

    def pool(slot, tl, d, ch):
        w = pltpu.roll(w_v[d], lax.rem(LANES - ch * 2 * BAG, LANES), 1)
        for octet in range(BAGS // 8):
            totals = [None, None]
            for j in range(BAG):
                picked = [None, None]
                for a in range(8):
                    r = ids[slot, tl, (octet * 8 + a) * BAG + j]
                    for h in range(2):
                        half = table if h == 0 else table.at[pl.ds(rows + GAP, rows)]
                        row = half[pl.ds(r, 8, stride=0), :]
                        picked[h] = row if a == 0 else jnp.where(sublane == a, row, picked[h])
                q = octet * BAG + j
                weight = jnp.broadcast_to(w[:, q : q + 1], (8, LANES))
                for h in range(2):
                    term = picked[h] * weight
                    totals[h] = term if j == 0 else totals[h] + term
            for h in range(2):
                obuf[d, ch, pl.ds((octet * 2 + h) * 8, 8), :] = totals[h]

    def step(t, _):
        for slot in range(2):
            i = t * 2 + slot
            ch, tg = piece_group(i)
            stage(i, slot).wait()
            for tl in range(8):
                d = tg * 8 + tl
                pool(slot, tl, d, ch)

                @pl.when(d != me)
                def _():
                    pltpu.make_async_remote_copy(
                        obuf.at[d, ch], got.at[ch, :, me], send_sem, recv_sem, device_id=(tg, tl), device_id_type=MESH
                    ).start()

            @pl.when(i + 2 < steps)
            def _():
                stage_next(i + 2, slot)

        return 0

    lax.fori_loop(0, steps // 2, step, 0)
    pltpu.make_async_copy(obuf.at[me], got.at[:, :, me], recv_sem).start()
    sent = obuf.at[pl.ds(0, peers - 1)]
    pltpu.make_async_copy(sent, sent, send_sem).wait()
    asked = ids_v.at[pl.ds(0, peers - 1)]
    pltpu.make_async_copy(asked, asked, ask_sem).wait()
    pltpu.make_async_copy(asked, asked, ask_sem).wait()
    pltpu.make_async_copy(got, got, recv_sem).wait()


def place_kernel(got, out_hbm, sem):
    parts = got.shape[0]

    def copy(p, h):
        return pltpu.make_async_copy(got.at[p, h], out_hbm.at[pl.ds(p * 8, 8), :, pl.ds(h * LANES, LANES)], sem.at[p, h])

    for p in range(parts):
        for h in range(2):
            copy(p, h).start()
    for p in range(parts):
        for h in range(2):
            copy(p, h).wait()


def body(ids, lengths, id_weights, table):
    examples, tables, bag = ids.shape
    pieces = examples // BAGS
    rows, width = table.shape
    slot = lax.broadcasted_iota(jnp.int32, ids.shape, 2)
    masked = jnp.where(slot < lengths[:, :, None], id_weights, jnp.zeros_like(id_weights))

    index = jnp.transpose(ids, (1, 0, 2)).reshape(tables, pieces, LANES)
    weights = masked.reshape(pieces * 2, 8, tables, bag)
    weights = jnp.transpose(weights, (2, 1, 0, 3)).reshape(tables, 8, LANES)
    got = pl.pallas_call(
        pool_send_kernel,
        out_shape=pltpu.VMEM((pieces, 2 * BAGS, tables, LANES), jnp.float32),
        in_specs=[ANY, ANY, HBM],
        out_specs=VMEM,
        scratch_shapes=[
            pltpu.VMEM((rows * 2 + GAP, LANES), jnp.float32),
            pltpu.VMEM((tables, pieces, 2 * BAGS, LANES), jnp.float32),
            pltpu.VMEM((tables, pieces, LANES), jnp.int32),
            pltpu.VMEM((tables, 8, LANES), jnp.float32),
            pltpu.SMEM((2, 8, LANES), jnp.int32),
            pltpu.SemaphoreType.DMA((2,)),
            pltpu.SemaphoreType.DMA((2,)),
            pltpu.SemaphoreType.DMA,
            pltpu.SemaphoreType.DMA((tables // 8,)),
            pltpu.SemaphoreType.DMA((tables // 8,)),
            pltpu.SemaphoreType.DMA,
            pltpu.SemaphoreType.DMA,
        ],
        compiler_params=pltpu.CompilerParams(vmem_limit_bytes=44 << 20, collective_id=0, has_side_effects=True),
        name="pool_send",
    )(index, weights, table)
    return pl.pallas_call(
        place_kernel,
        out_shape=jax.ShapeDtypeStruct((examples, tables, width), jnp.float32),
        in_specs=[VMEM],
        out_specs=ANY,
        scratch_shapes=[pltpu.SemaphoreType.DMA((examples // 8, 2))],
        compiler_params=pltpu.CompilerParams(vmem_limit_bytes=20 << 20),
        name="place",
    )(got.reshape(examples // 8, 2, 8, tables, LANES))


def solution(mesh):
    return jax.shard_map(body, mesh=mesh, in_specs=(SPEC,) * 4, out_specs=SPEC, check_vma=False)
```

```python
import jax
import jax.numpy as jnp
from jax import lax
from jax.experimental import pallas as pl
from jax.experimental.pallas import tpu as pltpu
from jax.sharding import PartitionSpec as P

MESH = pl.DeviceIdType.MESH
ANY = pl.BlockSpec(memory_space=pl.ANY)
HBM = pl.BlockSpec(memory_space=pltpu.HBM)
VMEM = pl.BlockSpec(memory_space=pltpu.VMEM)
SPEC = P(("group", "local"))
LANES = 128
BAG = 8
BAGS = 16
GAP = 8


def pool_send_kernel(
    ids_in, w_in, table_hbm, got, table, obuf, ids_v, w_v, ids, table_sem, stage_sem, ask_sem, ids_sem, w_sem, send_sem, recv_sem
):
    g, l = lax.axis_index("group"), lax.axis_index("local")
    me = g * 8 + l
    pieces, peers = got.shape[0], got.shape[2]
    groups = peers // 8
    steps = pieces * groups
    rows = table_hbm.shape[0]

    halves = [
        pltpu.make_async_copy(
            table_hbm.at[:, pl.ds(h * LANES, LANES)], table.at[pl.ds(h * (rows + GAP), rows)], table_sem.at[h]
        )
        for h in range(2)
    ]
    for half in halves:
        half.start()

    barrier = pltpu.get_barrier_semaphore()

    def greet(k, _):
        d = lax.rem(me + k, peers)
        pl.semaphore_signal(barrier, inc=1, device_id=(lax.div(d, 8), lax.rem(d, 8)), device_id_type=MESH)
        return 0

    lax.fori_loop(1, peers, greet, 0)

    gx, gz = lax.div(g, 4), lax.rem(g, 4)
    y, c = lax.div(l, 2), lax.rem(l, 2)
    pltpu.make_async_copy(ids_in.at[me], ids_v.at[g * 8], ids_sem.at[g]).start()
    pltpu.make_async_copy(w_in.at[me], w_v.at[g * 8], w_sem.at[g]).start()
    pl.semaphore_wait(barrier, peers - 1)

    def ask(i, _):
        ch = 0
        b = lax.rem(lax.rem(lax.div(i, 2), 8) * 5 + ch * 3, 8)
        q = lax.rem(lax.div(b, 4) + 2 * lax.rem(i, 2), 4) * 4 + lax.rem(lax.rem(b, 4) + 2 * lax.rem(i, 2), 4)
        tg = lax.rem(gx + 4 - lax.div(q, 4), 4) * 4 + lax.rem(gz + 4 - lax.rem(q, 4), 4)
        for r in range(8):
            tl = lax.rem(y + 4 - r // 2, 4) * 2 + lax.rem(c + r % 2, 2)
            d = tg * 8 + tl
            row = g * 8 + r

            @pl.when(d != me)
            def _():
                to = dict(device_id=(tg, tl), device_id_type=MESH)
                pltpu.make_async_remote_copy(ids_in.at[d], ids_v.at[row], ask_sem, ids_sem.at[g], **to).start()
                pltpu.make_async_remote_copy(w_in.at[d], w_v.at[row], ask_sem, w_sem.at[g], **to).start()

        return 0

    lax.fori_loop(0, groups, ask, 0)

    for half in halves:
        half.wait()

    def piece_group(i):
        ch = lax.div(i, groups)
        b = lax.rem(lax.rem(lax.div(i, 2), 8) * 5 + ch * 3, 8)
        q = lax.rem(lax.div(b, 4) + 2 * lax.rem(i, 2), 4) * 4 + lax.rem(lax.rem(b, 4) + 2 * lax.rem(i, 2), 4)
        return ch, lax.rem(gx + lax.div(q, 4), 4) * 4 + lax.rem(gz + lax.rem(q, 4), 4)

    def stage(i, slot):
        ch, tg = piece_group(i)
        return pltpu.make_async_copy(ids_v.at[pl.ds(tg * 8, 8), ch], ids.at[slot], stage_sem.at[slot])

    def stage_next(i, slot):
        @pl.when(i < groups)
        def _():
            _, tg = piece_group(i)
            block = ids_v.at[pl.ds(tg * 8, 8)]
            pltpu.make_async_copy(block, block, ids_sem.at[tg]).wait()
            block = w_v.at[pl.ds(tg * 8, 8)]
            pltpu.make_async_copy(block, block, w_sem.at[tg]).wait()

        stage(i, slot).start()

    stage_next(0, 0)
    stage_next(1, 1)

    sublane = lax.broadcasted_iota(jnp.int32, (8, LANES), 0)

    def pool(slot, tl, row_of, d, ch):
        w = pltpu.roll(w_v[row_of], lax.rem(LANES - ch * 2 * BAG, LANES), 1)
        for octet in range(BAGS // 8):
            totals = [None, None]
            for j in range(BAG):
                picked = [None, None]
                for a in range(8):
                    r = ids[slot, tl, (octet * 8 + a) * BAG + j]
                    for h in range(2):
                        half = table if h == 0 else table.at[pl.ds(rows + GAP, rows)]
                        row = half[pl.ds(r, 8, stride=0), :]
                        picked[h] = row if a == 0 else jnp.where(sublane == a, row, picked[h])
                q = octet * BAG + j
                weight = jnp.broadcast_to(w[:, q : q + 1], (8, LANES))
                for h in range(2):
                    term = picked[h] * weight
                    totals[h] = term if j == 0 else totals[h] + term
            for h in range(2):
                obuf[d, ch, pl.ds((octet * 2 + h) * 8, 8), :] = totals[h]

    def step(t, _):
        for slot in range(2):
            i = t * 2 + slot
            ch, tg = piece_group(i)
            stage(i, slot).wait()
            for r in (0, 3, 6, 1, 4, 7, 2, 5):
                tl = lax.rem(y + r // 2, 4) * 2 + lax.rem(c + r % 2, 2)
                d = tg * 8 + tl
                pool(slot, r, tg * 8 + r, d, ch)

                @pl.when(d != me)
                def _():
                    pltpu.make_async_remote_copy(
                        obuf.at[d, ch], got.at[ch, :, me], send_sem, recv_sem, device_id=(tg, tl), device_id_type=MESH
                    ).start()

            @pl.when(i + 2 < steps)
            def _():
                stage_next(i + 2, slot)

        return 0

    lax.fori_loop(0, steps // 2, step, 0)
    pltpu.make_async_copy(obuf.at[me], got.at[:, :, me], recv_sem).start()
    sent = obuf.at[pl.ds(0, peers - 1)]
    pltpu.make_async_copy(sent, sent, send_sem).wait()
    asked = ids_v.at[pl.ds(0, peers - 1)]
    pltpu.make_async_copy(asked, asked, ask_sem).wait()
    pltpu.make_async_copy(asked, asked, ask_sem).wait()
    pltpu.make_async_copy(got, got, recv_sem).wait()


def place_kernel(got, out_hbm, sem):
    parts = got.shape[0]

    def copy(p, h):
        return pltpu.make_async_copy(got.at[p, h], out_hbm.at[pl.ds(p * 8, 8), :, pl.ds(h * LANES, LANES)], sem.at[p, h])

    for p in range(parts):
        for h in range(2):
            copy(p, h).start()
    for p in range(parts):
        for h in range(2):
            copy(p, h).wait()


def body(ids, lengths, id_weights, table):
    examples, tables, bag = ids.shape
    pieces = examples // BAGS
    rows, width = table.shape
    slot = lax.broadcasted_iota(jnp.int32, ids.shape, 2)
    masked = jnp.where(slot < lengths[:, :, None], id_weights, jnp.zeros_like(id_weights))

    index = jnp.transpose(ids, (1, 0, 2)).reshape(tables, pieces, LANES)
    weights = masked.reshape(pieces * 2, 8, tables, bag)
    weights = jnp.transpose(weights, (2, 1, 0, 3)).reshape(tables, 8, LANES)
    got = pl.pallas_call(
        pool_send_kernel,
        out_shape=pltpu.VMEM((pieces, 2 * BAGS, tables, LANES), jnp.float32),
        in_specs=[ANY, ANY, HBM],
        out_specs=VMEM,
        scratch_shapes=[
            pltpu.VMEM((rows * 2 + GAP, LANES), jnp.float32),
            pltpu.VMEM((tables, pieces, 2 * BAGS, LANES), jnp.float32),
            pltpu.VMEM((tables, pieces, LANES), jnp.int32),
            pltpu.VMEM((tables, 8, LANES), jnp.float32),
            pltpu.SMEM((2, 8, LANES), jnp.int32),
            pltpu.SemaphoreType.DMA((2,)),
            pltpu.SemaphoreType.DMA((2,)),
            pltpu.SemaphoreType.DMA,
            pltpu.SemaphoreType.DMA((tables // 8,)),
            pltpu.SemaphoreType.DMA((tables // 8,)),
            pltpu.SemaphoreType.DMA,
            pltpu.SemaphoreType.DMA,
        ],
        compiler_params=pltpu.CompilerParams(vmem_limit_bytes=44 << 20, collective_id=0, has_side_effects=True),
        name="pool_send",
    )(index, weights, table)
    return pl.pallas_call(
        place_kernel,
        out_shape=jax.ShapeDtypeStruct((examples, tables, width), jnp.float32),
        in_specs=[VMEM],
        out_specs=ANY,
        scratch_shapes=[pltpu.SemaphoreType.DMA((examples // 8, 2))],
        compiler_params=pltpu.CompilerParams(vmem_limit_bytes=20 << 20),
        name="place",
    )(got.reshape(examples // 8, 2, 8, tables, LANES))


def solution(mesh):
    return jax.shard_map(body, mesh=mesh, in_specs=(SPEC,) * 4, out_specs=SPEC, check_vma=False)
```

```python
import jax
import jax.numpy as jnp
from jax import lax
from jax.experimental import pallas as pl
from jax.experimental.pallas import tpu as pltpu
from jax.sharding import PartitionSpec as P

MESH = pl.DeviceIdType.MESH
ANY = pl.BlockSpec(memory_space=pl.ANY)
HBM = pl.BlockSpec(memory_space=pltpu.HBM)
VMEM = pl.BlockSpec(memory_space=pltpu.VMEM)
SPEC = P(("group", "local"))
LANES = 128
BAG = 8
BAGS = 16
GAP = 8


def pool_send_kernel(
    ids_hbm, len_hbm, w_hbm, table_hbm, got, table, obuf, ids_e, len_e, w_e, ids_in, w_in, ids_v, w_v, ids, in_sem, table_sem, stage_sem, ask_sem, ids_sem, w_sem, send_sem, recv_sem
):
    g, l = lax.axis_index("group"), lax.axis_index("local")
    me = g * 8 + l
    pieces, peers = got.shape[0], got.shape[2]
    groups = peers // 8
    steps = pieces * groups
    rows = table_hbm.shape[0]

    halves = [
        pltpu.make_async_copy(
            table_hbm.at[:, pl.ds(h * LANES, LANES)], table.at[pl.ds(h * (rows + GAP), rows)], table_sem.at[h]
        )
        for h in range(2)
    ]
    inputs = [
        pltpu.make_async_copy(whole, here, in_sem.at[k])
        for k, (whole, here) in enumerate(((ids_hbm, ids_e), (len_hbm, len_e.at[pl.ds(0, len_hbm.shape[0])]), (w_hbm, w_e)))
    ]
    for copy in inputs + halves:
        copy.start()

    barrier = pltpu.get_barrier_semaphore()

    def greet(k, _):
        d = lax.rem(me + k, peers)
        pl.semaphore_signal(barrier, inc=1, device_id=(lax.div(d, 8), lax.rem(d, 8)), device_id_type=MESH)
        return 0

    lax.fori_loop(1, peers, greet, 0)

    gx, gz = lax.div(g, 4), lax.rem(g, 4)
    y, c = lax.div(l, 2), lax.rem(l, 2)
    for copy in inputs:
        copy.wait()

    sublane = lax.broadcasted_iota(jnp.int32, (8, LANES), 0)

    def turn(k, _):
        by_id = ids_e[pl.ds(pl.multiple_of(k * LANES, LANES), LANES), :].T
        live = []
        for p in range(LANES // 8):
            e = p * 8 + k
            weight = w_e[pl.ds(pl.multiple_of(e * 8, 8), 8), :]
            live.append(jnp.where(sublane < len_e[pl.ds(e, 8, stride=0), :], weight, jnp.zeros_like(weight)))
        by_weight = jnp.concatenate(live, axis=0).T
        for t in range(peers // 8):
            ids_in[pl.ds(t * 64 + k, 8, stride=8), :] = by_id[t * 8 : t * 8 + 8]
            w_in[pl.ds(t * 64 + k, 8, stride=8), :] = by_weight[t * 8 : t * 8 + 8]
        return 0

    lax.fori_loop(0, 8, turn, 0)

    def tile(ref, d):
        return ref.at[pl.ds(pl.multiple_of(d * 8, 8), 8)]

    pltpu.make_async_copy(tile(ids_in, me), ids_v.at[g * 8], ids_sem.at[g]).start()
    pltpu.make_async_copy(tile(w_in, me), w_v.at[g * 8], w_sem.at[g]).start()
    pl.semaphore_wait(barrier, peers - 1)

    def ask(i, _):
        ch = 0
        b = lax.rem(lax.rem(lax.div(i, 2), 8) * 5 + ch * 3, 8)
        q = lax.rem(lax.div(b, 4) + 2 * lax.rem(i, 2), 4) * 4 + lax.rem(lax.rem(b, 4) + 2 * lax.rem(i, 2), 4)
        tg = lax.rem(gx + 4 - lax.div(q, 4), 4) * 4 + lax.rem(gz + 4 - lax.rem(q, 4), 4)
        for r in range(8):
            tl = lax.rem(y + 4 - r // 2, 4) * 2 + lax.rem(c + r % 2, 2)
            d = tg * 8 + tl
            row = g * 8 + r

            @pl.when(d != me)
            def _():
                to = dict(device_id=(tg, tl), device_id_type=MESH)
                pltpu.make_async_remote_copy(tile(ids_in, d), ids_v.at[row], ask_sem, ids_sem.at[g], **to).start()
                pltpu.make_async_remote_copy(tile(w_in, d), w_v.at[row], ask_sem, w_sem.at[g], **to).start()

        return 0

    lax.fori_loop(0, groups, ask, 0)

    for half in halves:
        half.wait()

    def piece_group(i):
        ch = lax.div(i, groups)
        b = lax.rem(lax.rem(lax.div(i, 2), 8) * 5 + ch * 3, 8)
        q = lax.rem(lax.div(b, 4) + 2 * lax.rem(i, 2), 4) * 4 + lax.rem(lax.rem(b, 4) + 2 * lax.rem(i, 2), 4)
        return ch, lax.rem(gx + lax.div(q, 4), 4) * 4 + lax.rem(gz + lax.rem(q, 4), 4)

    def stage(i, slot):
        ch, tg = piece_group(i)
        return pltpu.make_async_copy(ids_v.at[pl.ds(tg * 8, 8), ch], ids.at[slot], stage_sem.at[slot])

    def stage_next(i, slot):
        @pl.when(i < groups)
        def _():
            _, tg = piece_group(i)
            block = ids_v.at[pl.ds(tg * 8, 8)]
            pltpu.make_async_copy(block, block, ids_sem.at[tg]).wait()
            block = w_v.at[pl.ds(tg * 8, 8)]
            pltpu.make_async_copy(block, block, w_sem.at[tg]).wait()

        stage(i, slot).start()

    stage_next(0, 0)
    stage_next(1, 1)

    def pool(slot, tl, row_of, d, ch):
        w = pltpu.roll(w_v[row_of], lax.rem(LANES - ch * 2 * BAG, LANES), 1)
        for octet in range(BAGS // 8):
            totals = [None, None]
            for j in range(BAG):
                picked = [None, None]
                for a in range(8):
                    r = ids[slot, tl, (octet * 8 + a) * BAG + j]
                    for h in range(2):
                        half = table if h == 0 else table.at[pl.ds(rows + GAP, rows + 8)]
                        row = half[pl.ds(r, 8, stride=0), :]
                        picked[h] = row if a == 0 else jnp.where(sublane == a, row, picked[h])
                q = octet * BAG + j
                weight = jnp.broadcast_to(w[:, q : q + 1], (8, LANES))
                for h in range(2):
                    term = picked[h] * weight
                    totals[h] = term if j == 0 else totals[h] + term
            for h in range(2):
                obuf[d, ch, pl.ds((octet * 2 + h) * 8, 8), :] = totals[h]

    def step(t, _):
        for slot in range(2):
            i = t * 2 + slot
            ch, tg = piece_group(i)
            stage(i, slot).wait()
            for r in (0, 3, 6, 1, 4, 7, 2, 5):
                tl = lax.rem(y + r // 2, 4) * 2 + lax.rem(c + r % 2, 2)
                d = tg * 8 + tl
                pool(slot, r, tg * 8 + r, d, ch)

                @pl.when(d != me)
                def _():
                    pltpu.make_async_remote_copy(
                        obuf.at[d, ch], got.at[ch, :, me], send_sem, recv_sem, device_id=(tg, tl), device_id_type=MESH
                    ).start()

            @pl.when(i + 2 < steps)
            def _():
                stage_next(i + 2, slot)

        return 0

    lax.fori_loop(0, steps // 2, step, 0)
    pltpu.make_async_copy(obuf.at[me], got.at[:, :, me], recv_sem).start()
    sent = obuf.at[pl.ds(0, peers - 1)]
    pltpu.make_async_copy(sent, sent, send_sem).wait()
    asked = ids_v.at[pl.ds(0, peers - 1)]
    pltpu.make_async_copy(asked, asked, ask_sem).wait()
    pltpu.make_async_copy(asked, asked, ask_sem).wait()
    pltpu.make_async_copy(got, got, recv_sem).wait()


def place_kernel(got, out_hbm, sem):
    parts = got.shape[0]

    def copy(p, h):
        return pltpu.make_async_copy(got.at[p, h], out_hbm.at[pl.ds(p * 8, 8), :, pl.ds(h * LANES, LANES)], sem.at[p, h])

    for p in range(parts):
        for h in range(2):
            copy(p, h).start()
    for p in range(parts):
        for h in range(2):
            copy(p, h).wait()


def body(ids, lengths, id_weights, table):
    examples, tables, bag = ids.shape
    pieces = examples // BAGS
    rows, width = table.shape

    def by_slot(v):
        return jnp.transpose(v, (0, 2, 1)).reshape(examples * bag, tables)

    got = pl.pallas_call(
        pool_send_kernel,
        out_shape=pltpu.VMEM((pieces, 2 * BAGS, tables, LANES), jnp.float32),
        in_specs=[HBM] * 4,
        out_specs=VMEM,
        scratch_shapes=[
            pltpu.VMEM((rows * 2 + GAP + 8, LANES), jnp.float32),
            pltpu.VMEM((tables, pieces, 2 * BAGS, LANES), jnp.float32),
            pltpu.VMEM((examples * bag, tables), jnp.int32),
            pltpu.VMEM((examples + 8, tables), jnp.int32),
            pltpu.VMEM((examples * bag, tables), jnp.float32),
            pltpu.VMEM((tables * pieces, LANES), jnp.int32),
            pltpu.VMEM((tables * 8, LANES), jnp.float32),
            pltpu.VMEM((tables, pieces, LANES), jnp.int32),
            pltpu.VMEM((tables, 8, LANES), jnp.float32),
            pltpu.SMEM((2, 8, LANES), jnp.int32),
            pltpu.SemaphoreType.DMA((3,)),
            pltpu.SemaphoreType.DMA((2,)),
            pltpu.SemaphoreType.DMA((2,)),
            pltpu.SemaphoreType.DMA,
            pltpu.SemaphoreType.DMA((tables // 8,)),
            pltpu.SemaphoreType.DMA((tables // 8,)),
            pltpu.SemaphoreType.DMA,
            pltpu.SemaphoreType.DMA,
        ],
        compiler_params=pltpu.CompilerParams(vmem_limit_bytes=44 << 20, collective_id=0, has_side_effects=True),
        name="pool_send",
    )(by_slot(ids), lengths, by_slot(id_weights), table)
    return pl.pallas_call(
        place_kernel,
        out_shape=jax.ShapeDtypeStruct((examples, tables, width), jnp.float32),
        in_specs=[VMEM],
        out_specs=ANY,
        scratch_shapes=[pltpu.SemaphoreType.DMA((examples // 8, 2))],
        compiler_params=pltpu.CompilerParams(vmem_limit_bytes=20 << 20),
        name="place",
    )(got.reshape(examples // 8, 2, 8, tables, LANES))


def solution(mesh):
    return jax.shard_map(body, mesh=mesh, in_specs=(SPEC,) * 4, out_specs=SPEC, check_vma=False)
```

```python
import jax
import jax.numpy as jnp
from jax import lax
from jax.experimental import pallas as pl
from jax.experimental.pallas import tpu as pltpu
from jax.sharding import PartitionSpec as P

MESH = pl.DeviceIdType.MESH
ANY = pl.BlockSpec(memory_space=pl.ANY)
HBM = pl.BlockSpec(memory_space=pltpu.HBM)
VMEM = pl.BlockSpec(memory_space=pltpu.VMEM)
SPEC = P(("group", "local"))
LANES = 128
BAG = 8
BAGS = 16
GAP = 8


def pool_send_kernel(
    ids_hbm, len_hbm, w_hbm, table_hbm, got, table, obuf, ids_e, len_e, w_e, ids_in, w_in, ids_v, w_v, ids, in_sem, table_sem, stage_sem, ask_sem, ids_sem, w_sem, send_sem, recv_sem
):
    g, l = lax.axis_index("group"), lax.axis_index("local")
    me = g * 8 + l
    pieces, peers = got.shape[0], got.shape[2]
    groups = peers // 8
    steps = pieces * groups
    rows = table_hbm.shape[0]

    halves = [
        pltpu.make_async_copy(
            table_hbm.at[:, pl.ds(h * LANES, LANES)], table.at[pl.ds(h * (rows + GAP), rows)], table_sem.at[h]
        )
        for h in range(2)
    ]
    inputs = [
        pltpu.make_async_copy(whole, here, in_sem.at[k])
        for k, (whole, here) in enumerate(((ids_hbm, ids_e), (len_hbm, len_e.at[pl.ds(0, len_hbm.shape[0])]), (w_hbm, w_e)))
    ]
    for copy in inputs + halves:
        copy.start()

    barrier = pltpu.get_barrier_semaphore()

    def greet(k, _):
        tg = lax.rem(g + k, groups)
        for tl in range(8):

            @pl.when(tg * 8 + tl != me)
            def _():
                pl.semaphore_signal(barrier, inc=1, device_id=(tg, tl), device_id_type=MESH)

        return 0

    lax.fori_loop(0, groups, greet, 0)

    gx, gz = lax.div(g, 4), lax.rem(g, 4)
    y, c = lax.div(l, 2), lax.rem(l, 2)
    for copy in inputs:
        copy.wait()

    sublane = lax.broadcasted_iota(jnp.int32, (8, LANES), 0)

    def turn(k, _):
        by_id = ids_e[pl.ds(pl.multiple_of(k * LANES, LANES), LANES), :].T
        live = []
        for p in range(LANES // 8):
            e = p * 8 + k
            weight = w_e[pl.ds(pl.multiple_of(e * 8, 8), 8), :]
            live.append(jnp.where(sublane < len_e[pl.ds(e, 8, stride=0), :], weight, jnp.zeros_like(weight)))
        by_weight = jnp.concatenate(live, axis=0).T
        for t in range(peers // 8):
            ids_in[pl.ds(t * 64 + k, 8, stride=8), :] = by_id[t * 8 : t * 8 + 8]
            w_in[pl.ds(t * 64 + k, 8, stride=8), :] = by_weight[t * 8 : t * 8 + 8]
        return 0

    lax.fori_loop(0, 8, turn, 0)

    def tile(ref, d):
        return ref.at[pl.ds(pl.multiple_of(d * 8, 8), 8)]

    pltpu.make_async_copy(tile(ids_in, me), ids_v.at[g * 8], ids_sem.at[g]).start()
    pltpu.make_async_copy(tile(w_in, me), w_v.at[g * 8], w_sem.at[g]).start()
    pl.semaphore_wait(barrier, peers - 1)

    def ask(i, _):
        ch = 0
        b = lax.rem(lax.rem(lax.div(i, 2), 8) * 7 + ch * 5, 8)
        q = lax.rem(lax.div(b, 4) + 2 * lax.rem(i, 2), 4) * 4 + lax.rem(lax.rem(b, 4) + 2 * lax.rem(i, 2), 4)
        tg = lax.rem(gx + 4 - lax.div(q, 4), 4) * 4 + lax.rem(gz + 4 - lax.rem(q, 4), 4)
        for r in range(8):
            tl = lax.rem(y + 4 - r // 2, 4) * 2 + lax.rem(c + r % 2, 2)
            d = tg * 8 + tl
            row = g * 8 + r

            @pl.when(d != me)
            def _():
                to = dict(device_id=(tg, tl), device_id_type=MESH)
                pltpu.make_async_remote_copy(tile(ids_in, d), ids_v.at[row], ask_sem, ids_sem.at[g], **to).start()
                pltpu.make_async_remote_copy(tile(w_in, d), w_v.at[row], ask_sem, w_sem.at[g], **to).start()

        return 0

    lax.fori_loop(0, groups, ask, 0)

    for half in halves:
        half.wait()

    def piece_group(i):
        ch = lax.div(i, groups)
        b = lax.rem(lax.rem(lax.div(i, 2), 8) * 7 + ch * 5, 8)
        q = lax.rem(lax.div(b, 4) + 2 * lax.rem(i, 2), 4) * 4 + lax.rem(lax.rem(b, 4) + 2 * lax.rem(i, 2), 4)
        return ch, lax.rem(gx + lax.div(q, 4), 4) * 4 + lax.rem(gz + lax.rem(q, 4), 4)

    def stage(i, slot):
        ch, tg = piece_group(i)
        return pltpu.make_async_copy(ids_v.at[pl.ds(tg * 8, 8), ch], ids.at[slot], stage_sem.at[slot])

    def stage_next(i, slot):
        @pl.when(i < groups)
        def _():
            _, tg = piece_group(i)
            block = ids_v.at[pl.ds(tg * 8, 8)]
            pltpu.make_async_copy(block, block, ids_sem.at[tg]).wait()
            block = w_v.at[pl.ds(tg * 8, 8)]
            pltpu.make_async_copy(block, block, w_sem.at[tg]).wait()

        stage(i, slot).start()

    stage_next(0, 0)
    stage_next(1, 1)

    def pool(slot, tl, row_of, d, ch):
        w = pltpu.roll(w_v[row_of], lax.rem(LANES - ch * 2 * BAG, LANES), 1)
        for octet in range(BAGS // 8):
            totals = [None, None]
            for j in range(BAG):
                picked = [None, None]
                for a in range(8):
                    r = ids[slot, tl, (octet * 8 + a) * BAG + j]
                    for h in range(2):
                        half = table if h == 0 else table.at[pl.ds(rows + GAP, rows + 8)]
                        row = half[pl.ds(r, 8, stride=0), :]
                        picked[h] = row if a == 0 else jnp.where(sublane == a, row, picked[h])
                q = octet * BAG + j
                weight = jnp.broadcast_to(w[:, q : q + 1], (8, LANES))
                for h in range(2):
                    term = picked[h] * weight
                    totals[h] = term if j == 0 else totals[h] + term
            for h in range(2):
                obuf[d, ch, pl.ds((octet * 2 + h) * 8, 8), :] = totals[h]

    def step(t, _):
        for slot in range(2):
            i = t * 2 + slot
            ch, tg = piece_group(i)
            stage(i, slot).wait()
            for r in (0, 3, 6, 1, 4, 7, 2, 5):
                tl = lax.rem(y + r // 2, 4) * 2 + lax.rem(c + r % 2, 2)
                d = tg * 8 + tl
                pool(slot, r, tg * 8 + r, d, ch)

                @pl.when(d != me)
                def _():
                    pltpu.make_async_remote_copy(
                        obuf.at[d, ch], got.at[ch, :, me], send_sem, recv_sem, device_id=(tg, tl), device_id_type=MESH
                    ).start()

            @pl.when(i + 2 < steps)
            def _():
                stage_next(i + 2, slot)

        return 0

    lax.fori_loop(0, steps // 2, step, 0)
    pltpu.make_async_copy(obuf.at[me], got.at[:, :, me], recv_sem).start()
    sent = obuf.at[pl.ds(0, peers - 1)]
    pltpu.make_async_copy(sent, sent, send_sem).wait()
    asked = ids_v.at[pl.ds(0, peers - 1)]
    pltpu.make_async_copy(asked, asked, ask_sem).wait()
    pltpu.make_async_copy(asked, asked, ask_sem).wait()
    pltpu.make_async_copy(got, got, recv_sem).wait()


def place_kernel(got, out_hbm, sem):
    parts = got.shape[0]

    def copy(p, h):
        return pltpu.make_async_copy(got.at[p, h], out_hbm.at[pl.ds(p * 8, 8), :, pl.ds(h * LANES, LANES)], sem.at[p, h])

    for p in range(parts):
        for h in range(2):
            copy(p, h).start()
    for p in range(parts):
        for h in range(2):
            copy(p, h).wait()


def body(ids, lengths, id_weights, table):
    examples, tables, bag = ids.shape
    pieces = examples // BAGS
    rows, width = table.shape

    def by_slot(v):
        return jnp.transpose(v, (0, 2, 1)).reshape(examples * bag, tables)

    got = pl.pallas_call(
        pool_send_kernel,
        out_shape=pltpu.VMEM((pieces, 2 * BAGS, tables, LANES), jnp.float32),
        in_specs=[HBM] * 4,
        out_specs=VMEM,
        scratch_shapes=[
            pltpu.VMEM((rows * 2 + GAP + 8, LANES), jnp.float32),
            pltpu.VMEM((tables, pieces, 2 * BAGS, LANES), jnp.float32),
            pltpu.VMEM((examples * bag, tables), jnp.int32),
            pltpu.VMEM((examples + 8, tables), jnp.int32),
            pltpu.VMEM((examples * bag, tables), jnp.float32),
            pltpu.VMEM((tables * pieces, LANES), jnp.int32),
            pltpu.VMEM((tables * 8, LANES), jnp.float32),
            pltpu.VMEM((tables, pieces, LANES), jnp.int32),
            pltpu.VMEM((tables, 8, LANES), jnp.float32),
            pltpu.SMEM((2, 8, LANES), jnp.int32),
            pltpu.SemaphoreType.DMA((3,)),
            pltpu.SemaphoreType.DMA((2,)),
            pltpu.SemaphoreType.DMA((2,)),
            pltpu.SemaphoreType.DMA,
            pltpu.SemaphoreType.DMA((tables // 8,)),
            pltpu.SemaphoreType.DMA((tables // 8,)),
            pltpu.SemaphoreType.DMA,
            pltpu.SemaphoreType.DMA,
        ],
        compiler_params=pltpu.CompilerParams(vmem_limit_bytes=44 << 20, collective_id=0, has_side_effects=True),
        name="pool_send",
    )(by_slot(ids), lengths, by_slot(id_weights), table)
    return pl.pallas_call(
        place_kernel,
        out_shape=jax.ShapeDtypeStruct((examples, tables, width), jnp.float32),
        in_specs=[VMEM],
        out_specs=ANY,
        scratch_shapes=[pltpu.SemaphoreType.DMA((examples // 8, 2))],
        compiler_params=pltpu.CompilerParams(vmem_limit_bytes=20 << 20),
        name="place",
    )(got.reshape(examples // 8, 2, 8, tables, LANES))


def solution(mesh):
    return jax.shard_map(body, mesh=mesh, in_specs=(SPEC,) * 4, out_specs=SPEC, check_vma=False)
```
